32 devices in a mesh: shot: 4 (over x, core), rcv: 8 (over z, y).
Axes of the slice: x: 2, y: 2, z: 4, core: 2. Of those that a mesh axis runs over, the one named last changes fastest.
Arguments:
- response: bfloat16 [128, 128, 64], P('shot', 'rcv'), may hold values from -0.0625 to 0.0625
- traces: bfloat16 [128, 64, 512], P('shot', 'rcv'), may hold values from -6 to 6
Outputs:
- multiples: bfloat16 [128, 64, 512], P('shot', 'rcv')
The draws below stay inside these ranges and needn't reach their ends.
All inputs are finite; a program needn't handle non-finite values.
Results may differ from the reference program's by a relative error of at most 0.001.
Values may be sent and summed in bfloat16 or wider, within the bound.
A program may use at most 256 MiB of HBM per device.

```python
import jax
import jax.numpy as jnp
from jax import lax

POSITIONS = 128
TAPS = 64
SAMPLES = 512
SHOTS = 128
RECEIVERS = 64


def block_scale(stream_key, dims, pieces, least, top_value):
    loudness = 1.0
    for dim, blocks in pieces:
        draws = jax.random.uniform(jax.random.fold_in(jax.random.fold_in(stream_key, 6), dim), (blocks,), jnp.float32, least / len(pieces), top_value / len(pieces))
        loudness = loudness * jnp.repeat(jnp.exp(draws), dims[dim] // blocks).reshape((-1,) + (1,) * (len(dims) - 1 - dim))
    return loudness


def centred(key, extent, scale, bound, cuts=(), kind=jnp.bfloat16):
    array = jax.random.normal(key, extent, jnp.float32) * scale
    if len(cuts) > 0:
        array = block_scale(key, extent, cuts, -0.22, 0.18) * array
    return jnp.clip(array, min=-bound, max=bound).astype(kind)


def setup_inputs(seed: int = 0) -> dict:
    key_list = jax.random.split(jax.random.key(seed), 3)
    return {
        "response": centred(key_list[0], (SHOTS, POSITIONS, TAPS), (POSITIONS * TAPS) ** -0.5, 0.0625, ((0, 4), (1, 8))),
        "traces": centred(key_list[1], (POSITIONS, RECEIVERS, SAMPLES), 1.0, 6.0, ((0, 4), (1, 8))),
    }


def reference(response, traces):
    padded = jnp.pad(traces, ((0, 0), (0, 0), (TAPS, 0)))
    flat_size = RECEIVERS * SAMPLES

    def add_tap(tap_index, running):
        lag = jnp.asarray(tap_index).astype(jnp.int32)
        shifted = lax.dynamic_slice_in_dim(padded, (TAPS - lag).astype(jnp.int32), SAMPLES, 2)
        column = lax.dynamic_slice_in_dim(response, lag, 1, 2)[:, :, 0]
        return running + jnp.dot(column, shifted.reshape(POSITIONS, flat_size), preferred_element_type=jnp.float32)

    running = lax.fori_loop(0, TAPS, add_tap, jnp.zeros((SHOTS, flat_size), jnp.float32))
    return running.reshape(SHOTS, RECEIVERS, SAMPLES).astype(jnp.bfloat16)
```

```python
import functools

import jax
import jax.numpy as jnp
from jax import lax
from jax.experimental import pallas as pl
from jax.experimental.pallas import tpu as pltpu
from jax.sharding import PartitionSpec as P

MESH = pl.DeviceIdType.MESH
LANES = 128
WIDTH = 256


def put(ref, value):
    for t in range(value.shape[1] // LANES):
        ref[t] = value[:, t * LANES : (t + 1) * LANES]


def put_rows(ref, start, count, stride, value):
    for t in range(value.shape[1] // LANES):
        ref[t, pl.ds(start, count, stride=stride), :] = value[:, t * LANES : (t + 1) * LANES]


def get(ref):
    return jnp.concatenate([ref[t] for t in range(ref.shape[0])], axis=1)


def get_rows(ref, start, count, stride):
    return jnp.concatenate(
        [ref[t, pl.ds(start, count, stride=stride), :] for t in range(ref.shape[0])], axis=1
    )


def prepare(response_ref, traces_ref, x_ref, g_ref, a_ref, z_ref, w_ref, b_ref, y_ref, h_ref):
    shots, rows_e, taps = response_ref.shape
    rows_d, rcv, samples = traces_ref.shape
    phases = WIDTH // shots
    blocks = samples // phases
    per_tile = LANES // shots
    tiles = taps // per_tile

    b_ref[:, :taps] = response_ref[...].astype(jnp.float32).reshape(shots * rows_e, taps)
    stacked = jnp.concatenate(
        [b_ref[pl.ds(k, shots, stride=rows_e), :] for k in range(rows_e)], axis=0
    )
    put(y_ref, stacked.T[:taps])
    by_tap = [get_rows(y_ref, m, tiles, per_tile) for m in range(per_tile)]
    for k in range(rows_e):
        h_ref[pl.ds(k, tiles, stride=rows_e), :] = jnp.concatenate(
            [v[:, k * shots : (k + 1) * shots] for v in by_tap], axis=1
        )
    g_ref[...] = h_ref[...].astype(jnp.bfloat16)

    put(a_ref, traces_ref[...].astype(jnp.float32).reshape(rows_d * rcv, samples))
    stacked = jnp.concatenate([get_rows(a_ref, r, rows_d, rcv) for r in range(rcv)], axis=0)
    put(z_ref, stacked.T)
    by_phase = [get_rows(z_ref, v, blocks, phases) for v in range(phases)]
    for r in range(rcv):
        row = jnp.concatenate([z[:, r * rows_d : (r + 1) * rows_d] for z in by_phase], axis=1)
        put_rows(w_ref, r, blocks, rcv, row)
    x_ref[...] = get(w_ref).astype(jnp.bfloat16)


def predict(
    n_shot, n_rcv, chunks, taps, shots, rcv, samples,
    x_ref, g_ref, o_ref,
    xland, gland, bands, even, odd, acc, z_ref, f_ref,
    xsend, xrecv, xfwd, gsend, grecv, gfwd,
):
    rows, width = x_ref.shape
    phases = WIDTH // shots
    blocks = samples // phases
    per_tile = LANES // shots
    tiles = taps // per_tile
    pad = phases // per_tile
    rows_d = width // phases
    rows_e = g_ref.shape[0] // tiles
    history = taps // phases
    ratio = rows_d // rows_e
    outer_d, outer_e = n_shot // 2, n_rcv // 2
    me_d, me_e = lax.axis_index("shot"), lax.axis_index("rcv")
    in_d, in_e = lax.rem(me_d, 2), lax.rem(me_e, 2)
    out_d, out_e = me_d // 2, me_e // 2
    mate_d = out_d * 2 + 1 - in_d
    mate_e = out_e * 2 + 1 - in_e

    def at_d(step):
        return lax.rem(out_d + step + outer_d, outer_d) * 2 + in_d

    def at_e(step):
        return lax.rem(out_e + step + outer_e, outer_e) * 2 + in_e

    barrier = pltpu.get_barrier_semaphore()
    peers = [(mate_d, me_e), (me_d, mate_e)]
    peers += [(at_d(i), me_e) for i in range(1, outer_d)]
    peers += [(me_d, at_e(i)) for i in range(1, outer_e)]
    for peer in peers:
        pl.semaphore_signal(barrier, inc=1, device_id=peer, device_id_type=MESH)
    pl.semaphore_wait(barrier, len(peers))

    part = rows // chunks

    def xcopy(src, owner, c, send, peer):
        piece = pl.ds(c * part, part)
        return pltpu.make_async_remote_copy(
            src_ref=src.at[piece],
            dst_ref=xland.at[owner, piece],
            send_sem=send,
            recv_sem=xrecv.at[owner, c],
            device_id=peer,
            device_id_type=MESH,
        )

    def gcopy(src, owner, send, peer):
        return pltpu.make_async_remote_copy(
            src_ref=src,
            dst_ref=gland.at[owner],
            send_sem=send,
            recv_sem=grecv.at[owner],
            device_id=peer,
            device_id_type=MESH,
        )

    pending = []

    def go(copy):
        copy.start()
        pending.append(copy)

    for i in range(1, outer_e):
        go(gcopy(g_ref, me_e, gsend.at[i], (me_d, at_e(i))))
    go(gcopy(g_ref, me_e, gsend.at[0], (me_d, mate_e)))
    for c in range(chunks):
        for i in range(1, outer_d):
            go(xcopy(x_ref, me_d, c, xsend.at[i, c], (at_d(i), me_e)))
    for c in range(chunks):
        go(xcopy(x_ref, me_d, c, xsend.at[0, c], (mate_d, me_e)))

    todo_g = [at_e(-i) for i in range(1, outer_e)]
    todo_x = [(i, at_d(-i), c) for c in range(chunks) for i in range(1, outer_d)]
    for n in range(max(len(todo_g), len(todo_x))):
        if n < len(todo_g):
            owner = todo_g[n]
            gcopy(gland.at[owner], owner, gfwd.at[n], (me_d, mate_e)).wait_recv()
            go(gcopy(gland.at[owner], owner, gfwd.at[n], (me_d, mate_e)))
        if n < len(todo_x):
            i, owner, c = todo_x[n]
            copy = xcopy(xland.at[owner], owner, c, xfwd.at[i, c], (mate_d, me_e))
            copy.wait_recv()
            go(copy)
    for i in range(outer_e):
        owner = lax.rem(out_e + i, outer_e) * 2 + 1 - in_e
        gcopy(g_ref, owner, gsend.at[0], (me_d, mate_e)).wait_recv()
    gland[me_e] = g_ref[...]

    blank = jnp.zeros((rows_e, LANES), jnp.bfloat16)
    for e in range(n_rcv):
        place = pl.ds((e % ratio) * rows_e, rows_e)
        held = gland[e]
        padded = [blank] * pad
        padded += [held[a * rows_e : (a + 1) * rows_e] for a in range(tiles)]
        padded += [blank] * (pad + 1)
        for a in range(tiles + 2 * pad):
            for q in range(per_tile):
                value = padded[a]
                if q > 0:
                    value = jnp.concatenate(
                        [padded[a][:, q * shots :], padded[a + 1][:, : q * shots]], axis=1
                    )
                bands[e // ratio, q, a, place, :] = value

    head = history * rcv
    even[pl.ds(0, head), :] = jnp.zeros((head, width), jnp.bfloat16)
    odd[pl.ds(0, head), :] = jnp.zeros((head, width), jnp.bfloat16)

    def add(owner, held, first):
        even[pl.ds(head, rows), :] = held
        odd[pl.ds(head - rcv, rows), :] = held
        left, right = [], []
        for v1 in range(history + 1):
            if v1 % 2 == 0:
                left.append(even[pl.ds(v1 * rcv, rows), :])
            else:
                left.append(odd[pl.ds((v1 - 1) * rcv, rows), :])
            for v0 in range(phases):
                start = taps - v1 * phases - v0 + phases
                a, q = start // per_tile, start % per_tile
                right.append(
                    jnp.concatenate([bands[owner, q, a + n] for n in range(pad)], axis=1)
                )
        product = jnp.dot(
            jnp.concatenate(left, axis=1),
            jnp.concatenate(right, axis=0),
            preferred_element_type=jnp.float32,
        )
        put(acc, product if first else get(acc) + product)

    add(me_d, x_ref[...], True)
    for step in range(outer_d):
        owners = [lax.rem(out_d + step, outer_d) * 2 + 1 - in_d]
        if step > 0:
            owners = [at_d(step)] + owners
        for n, owner in enumerate(owners):
            if step == 0 or n == 1:
                for c in range(chunks):
                    xcopy(x_ref, owner, c, xsend.at[0, c], (mate_d, me_e)).wait_recv()
            add(owner, xland[owner], False)

    by_rcv = [get_rows(acc, r, blocks, rcv) for r in range(rcv)]
    for u in range(phases):
        row = jnp.concatenate([v[:, u * shots : (u + 1) * shots] for v in by_rcv], axis=1)
        put_rows(z_ref, u, blocks, phases, row)
    turned = get(z_ref).T
    for r in range(rcv):
        put_rows(f_ref, r, shots, rcv, turned[r * shots : (r + 1) * shots])
    o_ref[...] = get(f_ref).reshape(shots, rcv, samples).astype(jnp.bfloat16)
    for copy in pending:
        copy.wait_send()


def shards(n_shot, n_rcv, response, traces):
    shots, rows_e, taps = response.shape
    rows_d, rcv, samples = traces.shape
    phases = WIDTH // shots
    blocks = samples // phases
    per_tile = LANES // shots
    tiles = taps // per_tile
    pad = phases // per_tile
    rows = blocks * rcv
    width = phases * rows_d
    chunks = 4
    f32, bf16 = jnp.float32, jnp.bfloat16

    def tiled(height, across):
        return pltpu.VMEM((across // LANES, height, LANES), f32)

    vmem = pl.BlockSpec(memory_space=pltpu.VMEM)
    x, g = pl.pallas_call(
        prepare,
        out_shape=(
            jax.ShapeDtypeStruct((rows, width), bf16),
            jax.ShapeDtypeStruct((tiles * rows_e, LANES), bf16),
        ),
        in_specs=[vmem] * 2,
        out_specs=(vmem, vmem),
        scratch_shapes=[
            tiled(rows_d * rcv, samples),
            tiled(samples, rcv * rows_d),
            tiled(rows, width),
            pltpu.VMEM((shots * rows_e, LANES), f32),
            tiled(taps, rows_e * shots),
            pltpu.VMEM((tiles * rows_e, LANES), f32),
        ],
    )(response, traces)
    outer_d, outer_e = n_shot // 2, n_rcv // 2
    head = taps // phases * rcv
    dma = pltpu.SemaphoreType.DMA
    return pl.pallas_call(
        functools.partial(predict, n_shot, n_rcv, chunks, taps, shots, rcv, samples),
        out_shape=jax.ShapeDtypeStruct((shots, rcv, samples), bf16),
        in_specs=[vmem] * 2,
        out_specs=vmem,
        scratch_shapes=[
            pltpu.VMEM((n_shot, rows, width), bf16),
            pltpu.VMEM((n_rcv, tiles * rows_e, LANES), bf16),
            pltpu.VMEM((n_shot, per_tile, tiles + 2 * pad, rows_d, LANES), bf16),
            pltpu.VMEM((rows + head, width), bf16),
            pltpu.VMEM((rows + head, width), bf16),
            tiled(rows, WIDTH),
            tiled(samples, rcv * shots),
            tiled(shots * rcv, samples),
            dma((outer_d, chunks)),
            dma((n_shot, chunks)),
            dma((outer_d, chunks)),
            dma((outer_e,)),
            dma((n_rcv,)),
            dma((outer_e,)),
        ],
        compiler_params=pltpu.CompilerParams(collective_id=0, has_side_effects=True),
    )(x, g)


def solution(mesh):
    placed = P("shot", "rcv", None)
    return jax.shard_map(
        functools.partial(shards, mesh.shape["shot"], mesh.shape["rcv"]),
        mesh=mesh, in_specs=(placed, placed), out_specs=placed, check_vma=False,
    )
```

```python
import functools

import jax
import jax.numpy as jnp
from jax import lax
from jax.experimental import pallas as pl
from jax.experimental.pallas import tpu as pltpu
from jax.sharding import PartitionSpec as P

MESH = pl.DeviceIdType.MESH
LANES = 128
WIDTH = 256


def put(ref, value):
    for t in range(value.shape[1] // LANES):
        ref[t] = value[:, t * LANES : (t + 1) * LANES]


def put_rows(ref, start, count, stride, value):
    for t in range(value.shape[1] // LANES):
        ref[t, pl.ds(start, count, stride=stride), :] = value[:, t * LANES : (t + 1) * LANES]


def get(ref):
    return jnp.concatenate([ref[t] for t in range(ref.shape[0])], axis=1)


def get_rows(ref, start, count, stride):
    return jnp.concatenate(
        [ref[t, pl.ds(start, count, stride=stride), :] for t in range(ref.shape[0])], axis=1
    )


def turn_response(response, b_ref, y_ref, h_ref):
    shots, rows_e, taps = response.shape
    per_tile = LANES // shots
    tiles = taps // per_tile
    b_ref[:, :taps] = response.astype(jnp.float32).reshape(shots * rows_e, taps)
    stacked = jnp.concatenate(
        [b_ref[pl.ds(k, shots, stride=rows_e), :] for k in range(rows_e)], axis=0
    )
    put(y_ref, stacked.T[:taps])
    by_tap = [get_rows(y_ref, m, tiles, per_tile) for m in range(per_tile)]
    for k in range(rows_e):
        h_ref[pl.ds(k, tiles, stride=rows_e), :] = jnp.concatenate(
            [v[:, k * shots : (k + 1) * shots] for v in by_tap], axis=1
        )
    return h_ref[...].astype(jnp.bfloat16)


def turn_traces(traces, phases, a_ref, z_ref, w_ref):
    rows_d, rcv, samples = traces.shape
    blocks = samples // phases
    put(a_ref, traces.astype(jnp.float32).reshape(rows_d * rcv, samples))
    stacked = jnp.concatenate([get_rows(a_ref, r, rows_d, rcv) for r in range(rcv)], axis=0)
    put(z_ref, stacked.T)
    by_phase = [get_rows(z_ref, v, blocks, phases) for v in range(phases)]
    for r in range(rcv):
        row = jnp.concatenate([z[:, r * rows_d : (r + 1) * rows_d] for z in by_phase], axis=1)
        put_rows(w_ref, r, blocks, rcv, row)
    return get(w_ref).astype(jnp.bfloat16)


def arrange(y_ref, o_ref, acc, z_ref, f_ref):
    shots, rcv, samples = o_ref.shape
    phases = WIDTH // shots
    blocks = samples // phases
    put(acc, y_ref[...].astype(jnp.float32))
    by_rcv = [get_rows(acc, r, blocks, rcv) for r in range(rcv)]
    for u in range(phases):
        row = jnp.concatenate([v[:, u * shots : (u + 1) * shots] for v in by_rcv], axis=1)
        put_rows(z_ref, u, blocks, phases, row)
    turned = get(z_ref).T
    for r in range(rcv):
        put_rows(f_ref, r, shots, rcv, turned[r * shots : (r + 1) * shots])
    o_ref[...] = get(f_ref).reshape(shots, rcv, samples).astype(jnp.bfloat16)


def predict(
    n_shot, n_rcv, chunks,
    response_hbm, traces_hbm, o_ref,
    response_ref, traces_ref, b_ref, y_ref, h_ref, a_ref, z_ref, w_ref,
    x_ref, g_ref, xland, gland, bands, even, odd, acc,
    load, xsend, xrecv, xfwd, gsend, grecv, gfwd,
):
    shots, rows_e, taps = response_ref.shape
    rows_d, rcv, samples = traces_ref.shape
    rows, width = x_ref.shape
    phases = WIDTH // shots
    per_tile = LANES // shots
    tiles = taps // per_tile
    pad = phases // per_tile
    history = taps // phases
    ratio = rows_d // rows_e
    head = history * rcv
    half = rows // 2
    outer_d, outer_e = n_shot // 2, n_rcv // 2
    me_d, me_e = lax.axis_index("shot"), lax.axis_index("rcv")
    in_d, in_e = lax.rem(me_d, 2), lax.rem(me_e, 2)
    out_d, out_e = me_d // 2, me_e // 2
    mate_d = out_d * 2 + 1 - in_d
    mate_e = out_e * 2 + 1 - in_e

    def at_d(step):
        return lax.rem(out_d + step + outer_d, outer_d) * 2 + in_d

    def at_e(step):
        return lax.rem(out_e + step + outer_e, outer_e) * 2 + in_e

    barrier = pltpu.get_barrier_semaphore()
    peers = [(mate_d, me_e), (me_d, mate_e)]
    peers += [(at_d(i), me_e) for i in range(1, outer_d)]
    peers += [(me_d, at_e(i)) for i in range(1, outer_e)]
    for peer in peers:
        pl.semaphore_signal(barrier, inc=1, device_id=peer, device_id_type=MESH)
    fetch_r = pltpu.make_async_copy(response_hbm, response_ref, load.at[0])
    fetch_t = pltpu.make_async_copy(traces_hbm, traces_ref, load.at[1])
    fetch_r.start()
    fetch_t.start()

    part = rows // chunks

    def xcopy(src, owner, c, send, peer):
        piece = pl.ds(c * part, part)
        return pltpu.make_async_remote_copy(
            src_ref=src.at[piece],
            dst_ref=xland.at[owner, piece],
            send_sem=send,
            recv_sem=xrecv.at[owner, c],
            device_id=peer,
            device_id_type=MESH,
        )

    def gcopy(src, owner, send, peer):
        return pltpu.make_async_remote_copy(
            src_ref=src,
            dst_ref=gland.at[owner],
            send_sem=send,
            recv_sem=grecv.at[owner],
            device_id=peer,
            device_id_type=MESH,
        )

    pending = []

    def go(copy):
        copy.start()
        pending.append(copy)

    fetch_r.wait()
    g_ref[...] = turn_response(response_ref[...], b_ref, y_ref, h_ref)
    pl.semaphore_wait(barrier, len(peers))
    for i in range(1, outer_e):
        go(gcopy(g_ref, me_e, gsend.at[i], (me_d, at_e(i))))
    go(gcopy(g_ref, me_e, gsend.at[0], (me_d, mate_e)))
    fetch_t.wait()
    x_ref[...] = turn_traces(traces_ref[...], phases, a_ref, z_ref, w_ref)
    for c in range(chunks):
        for i in range(1, outer_d):
            go(xcopy(x_ref, me_d, c, xsend.at[i, c], (at_d(i), me_e)))
    for c in range(chunks):
        go(xcopy(x_ref, me_d, c, xsend.at[0, c], (mate_d, me_e)))

    blank = jnp.zeros((rows_e, LANES), jnp.bfloat16)

    def build(e, held):
        padded = [blank] * pad
        padded += [held[a * rows_e : (a + 1) * rows_e] for a in range(tiles)]
        padded += [blank] * (pad + 1)
        for a in range(tiles + 2 * pad):
            for q in range(per_tile):
                value = padded[a]
                if q > 0:
                    value = jnp.concatenate(
                        [padded[a][:, q * shots :], padded[a + 1][:, : q * shots]], axis=1
                    )
                bands[e, q, a] = value

    def place(owner, held, h):
        even[owner, pl.ds(head + h * half, half), :] = held
        odd[owner, pl.ds(head - rcv + h * half, half), :] = held

    def add(owner, h, first=False, last=False):
        left, right = [], []
        for v1 in range(history + 1):
            if v1 % 2 == 0:
                left.append(even[owner, pl.ds(h * half + v1 * rcv, half), :])
            else:
                left.append(odd[owner, pl.ds(h * half + (v1 - 1) * rcv, half), :])
            for v0 in range(phases):
                start = taps - v1 * phases - v0 + phases
                a, q = start // per_tile, start % per_tile
                for k in range(ratio):
                    e = owner * ratio + k
                    right.append(
                        jnp.concatenate([bands[e, q, a + n] for n in range(pad)], axis=1)
                    )
        total = jnp.dot(
            jnp.concatenate(left, axis=1),
            jnp.concatenate(right, axis=0),
            preferred_element_type=jnp.float32,
        )
        mine = pl.ds(h * half, half)
        if not first:
            total = acc[mine, :] + total
        if last:
            o_ref[mine, :] = total.astype(jnp.bfloat16)
        else:
            acc[mine, :] = total

    def forward_x(i, c):
        owner = at_d(-i)
        copy = xcopy(xland.at[owner], owner, c, xfwd.at[i, c], (mate_d, me_e))
        copy.wait_recv()
        go(copy)

    for d in range(n_shot):
        even[d, pl.ds(0, head), :] = jnp.zeros((head, width), jnp.bfloat16)
        odd[d, pl.ds(0, head), :] = jnp.zeros((head, width), jnp.bfloat16)
    for h in range(2):
        place(me_d, x_ref[pl.ds(h * half, half), :], h)
    build(me_e, g_ref[...])

    todo = [(i, c) for c in range(chunks) for i in range(1, outer_d)]
    late = [t for t in todo if t[1] == chunks - 1]
    todo = [t for t in todo if t[1] < chunks - 1]
    for n in range(max(outer_e - 1, len(todo))):
        if n < outer_e - 1:
            owner = at_e(-n - 1)
            copy = gcopy(gland.at[owner], owner, gfwd.at[n], (me_d, mate_e))
            copy.wait_recv()
            go(copy)
        if n < len(todo):
            forward_x(*todo[n])
        if n < outer_e - 1:
            build(owner, gland[owner])
    for i in range(outer_e):
        owner = lax.rem(out_e - i + outer_e, outer_e) * 2 + 1 - in_e
        gcopy(g_ref, owner, gsend.at[0], (me_d, mate_e)).wait_recv()
        build(owner, gland[owner])

    def arrived(owner, h):
        for c in range(h * chunks // 2, (h + 1) * chunks // 2):
            xcopy(x_ref, owner, c, xsend.at[0, c], (mate_d, me_e)).wait_recv()

    def bring(owner, h):
        place(owner, xland[owner, pl.ds(h * half, half), :], h)

    add(me_d, 0, first=True)
    for t in late:
        forward_x(*t)
    add(me_d, 1, first=True)
    for h in range(2):
        arrived(mate_d, h)
        bring(mate_d, h)
        add(mate_d, h)
    for h in range(2):
        for i in range(1, outer_d):
            bring(at_d(-i), h)
            add(at_d(-i), h)
        for i in range(1, outer_d):
            owner = lax.rem(out_d - i + outer_d, outer_d) * 2 + 1 - in_d
            arrived(owner, h)
            bring(owner, h)
            add(owner, h, last=i == outer_d - 1)
    for copy in pending:
        copy.wait_send()


def shards(n_shot, n_rcv, response, traces):
    shots, rows_e, taps = response.shape
    rows_d, rcv, samples = traces.shape
    phases = WIDTH // shots
    blocks = samples // phases
    per_tile = LANES // shots
    tiles = taps // per_tile
    pad = phases // per_tile
    rows = blocks * rcv
    width = phases * rows_d
    chunks = 4
    f32, bf16 = jnp.float32, jnp.bfloat16

    def tiled(height, across):
        return pltpu.VMEM((across // LANES, height, LANES), f32)

    vmem = pl.BlockSpec(memory_space=pltpu.VMEM)
    outer_d, outer_e = n_shot // 2, n_rcv // 2
    head = taps // phases * rcv
    dma = pltpu.SemaphoreType.DMA
    y = pl.pallas_call(
        functools.partial(predict, n_shot, n_rcv, chunks),
        out_shape=jax.ShapeDtypeStruct((rows, WIDTH), bf16),
        in_specs=[pl.BlockSpec(memory_space=pl.ANY)] * 2,
        out_specs=vmem,
        scratch_shapes=[
            pltpu.VMEM(response.shape, bf16),
            pltpu.VMEM(traces.shape, bf16),
            pltpu.VMEM((shots * rows_e, LANES), f32),
            tiled(taps, rows_e * shots),
            pltpu.VMEM((tiles * rows_e, LANES), f32),
            tiled(rows_d * rcv, samples),
            tiled(samples, rcv * rows_d),
            tiled(rows, width),
            pltpu.VMEM((rows, width), bf16),
            pltpu.VMEM((tiles * rows_e, LANES), bf16),
            pltpu.VMEM((n_shot, rows, width), bf16),
            pltpu.VMEM((n_rcv, tiles * rows_e, LANES), bf16),
            pltpu.VMEM((n_rcv, per_tile, tiles + 2 * pad, rows_e, LANES), bf16),
            pltpu.VMEM((n_shot, rows + head, width), bf16),
            pltpu.VMEM((n_shot, rows + head, width), bf16),
            pltpu.VMEM((rows, WIDTH), f32),
            dma((2,)),
            dma((outer_d, chunks)),
            dma((n_shot, chunks)),
            dma((outer_d, chunks)),
            dma((outer_e,)),
            dma((n_rcv,)),
            dma((outer_e,)),
        ],
        compiler_params=pltpu.CompilerParams(collective_id=0, has_side_effects=True),
    )(response, traces)
    return pl.pallas_call(
        arrange,
        out_shape=jax.ShapeDtypeStruct((shots, rcv, samples), bf16),
        in_specs=[vmem],
        out_specs=vmem,
        scratch_shapes=[
            tiled(rows, WIDTH),
            tiled(samples, rcv * shots),
            tiled(shots * rcv, samples),
        ],
    )(y)


def solution(mesh):
    placed = P("shot", "rcv", None)
    return jax.shard_map(
        functools.partial(shards, mesh.shape["shot"], mesh.shape["rcv"]),
        mesh=mesh, in_specs=(placed, placed), out_specs=placed, check_vma=False,
    )
```

```python
import functools

import jax
import jax.numpy as jnp
from jax import lax
from jax.experimental import pallas as pl
from jax.experimental.pallas import tpu as pltpu
from jax.sharding import PartitionSpec as P

MESH = pl.DeviceIdType.MESH
LANES = 128
WIDTH = 256


def put(ref, value):
    for t in range(value.shape[1] // LANES):
        ref[t] = value[:, t * LANES : (t + 1) * LANES]


def put_rows(ref, start, count, stride, value):
    for t in range(value.shape[1] // LANES):
        ref[t, pl.ds(start, count, stride=stride), :] = value[:, t * LANES : (t + 1) * LANES]


def get(ref):
    return jnp.concatenate([ref[t] for t in range(ref.shape[0])], axis=1)


def get_rows(ref, start, count, stride):
    return jnp.concatenate(
        [ref[t, pl.ds(start, count, stride=stride), :] for t in range(ref.shape[0])], axis=1
    )


def turn_response(response, b_ref, y_ref, h_ref):
    shots, rows_e, taps = response.shape
    per_tile = LANES // shots
    tiles = taps // per_tile
    b_ref[:, :taps] = response.astype(jnp.float32).reshape(shots * rows_e, taps)
    stacked = jnp.concatenate(
        [b_ref[pl.ds(k, shots, stride=rows_e), :] for k in range(rows_e)], axis=0
    )
    put(y_ref, stacked.T[:taps])
    by_tap = [get_rows(y_ref, m, tiles, per_tile) for m in range(per_tile)]
    for k in range(rows_e):
        h_ref[pl.ds(k, tiles, stride=rows_e), :] = jnp.concatenate(
            [v[:, k * shots : (k + 1) * shots] for v in by_tap], axis=1
        )
    return h_ref[...].astype(jnp.bfloat16)


def turn_traces(traces, phases, a_ref, z_ref, w_ref):
    rows_d, rcv, samples = traces.shape
    blocks = samples // phases
    put(a_ref, traces.astype(jnp.float32).reshape(rows_d * rcv, samples))
    stacked = jnp.concatenate([get_rows(a_ref, r, rows_d, rcv) for r in range(rcv)], axis=0)
    put(z_ref, stacked.T)
    by_phase = [get_rows(z_ref, v, blocks, phases) for v in range(phases)]
    for r in range(rcv):
        row = jnp.concatenate([z[:, r * rows_d : (r + 1) * rows_d] for z in by_phase], axis=1)
        put_rows(w_ref, r, blocks, rcv, row)
    return get(w_ref).astype(jnp.bfloat16)


def arrange(y_ref, o_ref, acc, z_ref, f_ref):
    shots, rcv, samples = o_ref.shape
    phases = WIDTH // shots
    blocks = samples // phases
    put(acc, y_ref[...].astype(jnp.float32))
    by_rcv = [get_rows(acc, r, blocks, rcv) for r in range(rcv)]
    for u in range(phases):
        row = jnp.concatenate([v[:, u * shots : (u + 1) * shots] for v in by_rcv], axis=1)
        put_rows(z_ref, u, blocks, phases, row)
    turned = get(z_ref).T
    for r in range(rcv):
        put_rows(f_ref, r, shots, rcv, turned[r * shots : (r + 1) * shots])
    o_ref[...] = get(f_ref).reshape(shots, rcv, samples).astype(jnp.bfloat16)


def predict(
    n_shot, n_rcv, chunks,
    response_hbm, traces_hbm, o_ref,
    response_ref, traces_ref, b_ref, y_ref, h_ref, a_ref, z_ref, w_ref,
    x_ref, g_ref, xland, gland, bands, even, odd, acc,
    load, xsend, xrecv, xfwd, gsend, grecv, gfwd,
):
    shots, rows_e, taps = response_ref.shape
    rows_d, rcv, samples = traces_ref.shape
    rows, width = x_ref.shape
    phases = WIDTH // shots
    per_tile = LANES // shots
    tiles = taps // per_tile
    pad = phases // per_tile
    history = taps // phases
    ratio = rows_d // rows_e
    head = history * rcv
    half = rows // 2
    outer_d, outer_e = n_shot // 2, n_rcv // 2
    me_d, me_e = lax.axis_index("shot"), lax.axis_index("rcv")
    in_d, in_e = lax.rem(me_d, 2), lax.rem(me_e, 2)
    out_d, out_e = me_d // 2, me_e // 2
    mate_d = out_d * 2 + 1 - in_d
    mate_e = out_e * 2 + 1 - in_e

    def at_d(step):
        return lax.rem(out_d + step + outer_d, outer_d) * 2 + in_d

    def at_e(step):
        return lax.rem(out_e + step + outer_e, outer_e) * 2 + in_e

    barrier = pltpu.get_barrier_semaphore()
    peers = [(mate_d, me_e), (me_d, mate_e)]
    peers += [(at_d(i), me_e) for i in range(1, outer_d)]
    peers += [(me_d, at_e(i)) for i in range(1, outer_e)]
    for peer in peers:
        pl.semaphore_signal(barrier, inc=1, device_id=peer, device_id_type=MESH)
    fetch_r = pltpu.make_async_copy(response_hbm, response_ref, load.at[0])
    fetch_t = pltpu.make_async_copy(traces_hbm, traces_ref, load.at[1])
    fetch_r.start()
    fetch_t.start()

    part = rows // chunks

    def xcopy(src, owner, c, send, peer):
        piece = pl.ds(c * part, part)
        return pltpu.make_async_remote_copy(
            src_ref=src.at[piece],
            dst_ref=xland.at[owner, piece],
            send_sem=send,
            recv_sem=xrecv.at[owner, c],
            device_id=peer,
            device_id_type=MESH,
        )

    def gcopy(src, owner, send, peer):
        return pltpu.make_async_remote_copy(
            src_ref=src,
            dst_ref=gland.at[owner],
            send_sem=send,
            recv_sem=grecv.at[owner],
            device_id=peer,
            device_id_type=MESH,
        )

    pending = []

    def go(copy):
        copy.start()
        pending.append(copy)

    fetch_r.wait()
    g_ref[...] = turn_response(response_ref[...], b_ref, y_ref, h_ref)
    pl.semaphore_wait(barrier, len(peers))
    order = sorted(range(1, outer_e), key=lambda i: abs(2 * i - outer_e))
    for i in order:
        go(gcopy(g_ref, me_e, gsend.at[i], (me_d, at_e(i))))
    go(gcopy(g_ref, me_e, gsend.at[0], (me_d, mate_e)))
    fetch_t.wait()
    x_ref[...] = turn_traces(traces_ref[...], phases, a_ref, z_ref, w_ref)
    for c in range(chunks):
        for i in range(1, outer_d):
            go(xcopy(x_ref, me_d, c, xsend.at[i, c], (at_d(i), me_e)))
    for c in range(chunks):
        go(xcopy(x_ref, me_d, c, xsend.at[0, c], (mate_d, me_e)))

    blank = jnp.zeros((rows_e, LANES), jnp.bfloat16)

    def build(e, held):
        padded = [blank] * pad
        padded += [held[a * rows_e : (a + 1) * rows_e] for a in range(tiles)]
        padded += [blank] * (pad + 1)
        for a in range(tiles + 2 * pad):
            for q in range(per_tile):
                value = padded[a]
                if q > 0:
                    value = jnp.concatenate(
                        [padded[a][:, q * shots :], padded[a + 1][:, : q * shots]], axis=1
                    )
                bands[e, q, a] = value

    def place(owner, held, h):
        even[owner, pl.ds(head + h * half, half), :] = held
        odd[owner, pl.ds(head - rcv + h * half, half), :] = held

    def add(owner, h, first=False, last=False):
        left, right = [], []
        for v1 in range(history + 1):
            if v1 % 2 == 0:
                left.append(even[owner, pl.ds(h * half + v1 * rcv, half), :])
            else:
                left.append(odd[owner, pl.ds(h * half + (v1 - 1) * rcv, half), :])
            for v0 in range(phases):
                start = taps - v1 * phases - v0 + phases
                a, q = start // per_tile, start % per_tile
                for k in range(ratio):
                    e = owner * ratio + k
                    right.append(
                        jnp.concatenate([bands[e, q, a + n] for n in range(pad)], axis=1)
                    )
        total = jnp.dot(
            jnp.concatenate(left, axis=1),
            jnp.concatenate(right, axis=0),
            preferred_element_type=jnp.float32,
        )
        mine = pl.ds(h * half, half)
        if not first:
            total = acc[mine, :] + total
        if last:
            o_ref[mine, :] = total.astype(jnp.bfloat16)
        else:
            acc[mine, :] = total

    def forward_x(i, c):
        owner = at_d(-i)
        copy = xcopy(xland.at[owner], owner, c, xfwd.at[i, c], (mate_d, me_e))
        copy.wait_recv()
        go(copy)

    for d in range(n_shot):
        even[d, pl.ds(0, head), :] = jnp.zeros((head, width), jnp.bfloat16)
        odd[d, pl.ds(0, head), :] = jnp.zeros((head, width), jnp.bfloat16)
    for h in range(2):
        place(me_d, x_ref[pl.ds(h * half, half), :], h)
    build(me_e, g_ref[...])

    def arrived(owner):
        for c in range(chunks):
            xcopy(x_ref, owner, c, xsend.at[0, c], (mate_d, me_e)).wait_recv()

    def bring(owner):
        for h in range(2):
            place(owner, xland[owner, pl.ds(h * half, half), :], h)

    todo = [(i, c) for c in range(chunks) for i in range(1, outer_d)]
    for n in range(max(outer_e - 1, len(todo))):
        if n < outer_e - 1:
            owner = at_e(-order[n])
            copy = gcopy(gland.at[owner], owner, gfwd.at[n], (me_d, mate_e))
            copy.wait_recv()
            go(copy)
        if n < len(todo):
            forward_x(*todo[n])
        if n < outer_e - 1:
            build(owner, gland[owner])
    arrived(mate_d)
    bring(mate_d)
    for i in range(1, outer_d):
        bring(at_d(-i))
    for i in range(1, outer_d):
        owner = lax.rem(out_d - i + outer_d, outer_d) * 2 + 1 - in_d
        arrived(owner)
        bring(owner)

    for n, i in enumerate([0] + order):
        group = lax.rem(out_e - i + outer_e, outer_e)
        owner = group * 2 + 1 - in_e
        gcopy(g_ref, owner, gsend.at[0], (me_d, mate_e)).wait_recv()
        build(owner, gland[owner])
        if ratio == 2:
            for h in range(2):
                add(group, h, first=n == 0, last=n == outer_e - 1)
    if ratio != 2:
        for d in range(n_shot):
            for h in range(2):
                add(d, h, first=d == 0, last=d == n_shot - 1)
    for copy in pending:
        copy.wait_send()


def shards(n_shot, n_rcv, response, traces):
    shots, rows_e, taps = response.shape
    rows_d, rcv, samples = traces.shape
    phases = WIDTH // shots
    blocks = samples // phases
    per_tile = LANES // shots
    tiles = taps // per_tile
    pad = phases // per_tile
    rows = blocks * rcv
    width = phases * rows_d
    chunks = 4
    f32, bf16 = jnp.float32, jnp.bfloat16

    def tiled(height, across):
        return pltpu.VMEM((across // LANES, height, LANES), f32)

    vmem = pl.BlockSpec(memory_space=pltpu.VMEM)
    outer_d, outer_e = n_shot // 2, n_rcv // 2
    head = taps // phases * rcv
    dma = pltpu.SemaphoreType.DMA
    y = pl.pallas_call(
        functools.partial(predict, n_shot, n_rcv, chunks),
        out_shape=jax.ShapeDtypeStruct((rows, WIDTH), bf16),
        in_specs=[pl.BlockSpec(memory_space=pl.ANY)] * 2,
        out_specs=vmem,
        scratch_shapes=[
            pltpu.VMEM(response.shape, bf16),
            pltpu.VMEM(traces.shape, bf16),
            pltpu.VMEM((shots * rows_e, LANES), f32),
            tiled(taps, rows_e * shots),
            pltpu.VMEM((tiles * rows_e, LANES), f32),
            tiled(rows_d * rcv, samples),
            tiled(samples, rcv * rows_d),
            tiled(rows, width),
            pltpu.VMEM((rows, width), bf16),
            pltpu.VMEM((tiles * rows_e, LANES), bf16),
            pltpu.VMEM((n_shot, rows, width), bf16),
            pltpu.VMEM((n_rcv, tiles * rows_e, LANES), bf16),
            pltpu.VMEM((n_rcv, per_tile, tiles + 2 * pad, rows_e, LANES), bf16),
            pltpu.VMEM((n_shot, rows + head, width), bf16),
            pltpu.VMEM((n_shot, rows + head, width), bf16),
            pltpu.VMEM((rows, WIDTH), f32),
            dma((2,)),
            dma((outer_d, chunks)),
            dma((n_shot, chunks)),
            dma((outer_d, chunks)),
            dma((outer_e,)),
            dma((n_rcv,)),
            dma((outer_e,)),
        ],
        compiler_params=pltpu.CompilerParams(collective_id=0, has_side_effects=True),
    )(response, traces)
    return pl.pallas_call(
        arrange,
        out_shape=jax.ShapeDtypeStruct((shots, rcv, samples), bf16),
        in_specs=[vmem],
        out_specs=vmem,
        scratch_shapes=[
            tiled(rows, WIDTH),
            tiled(samples, rcv * shots),
            tiled(shots * rcv, samples),
        ],
    )(y)


def solution(mesh):
    placed = P("shot", "rcv", None)
    return jax.shard_map(
        functools.partial(shards, mesh.shape["shot"], mesh.shape["rcv"]),
        mesh=mesh, in_specs=(placed, placed), out_specs=placed, check_vma=False,
    )
```

```python
import functools

import jax
import jax.numpy as jnp
from jax import lax
from jax.experimental import pallas as pl
from jax.experimental.pallas import tpu as pltpu
from jax.sharding import PartitionSpec as P

MESH = pl.DeviceIdType.MESH
LANES = 128
WIDTH = 256


def put(ref, value):
    for t in range(value.shape[1] // LANES):
        ref[t] = value[:, t * LANES : (t + 1) * LANES]


def put_rows(ref, start, count, stride, value):
    for t in range(value.shape[1] // LANES):
        ref[t, pl.ds(start, count, stride=stride), :] = value[:, t * LANES : (t + 1) * LANES]


def get(ref):
    return jnp.concatenate([ref[t] for t in range(ref.shape[0])], axis=1)


def get_rows(ref, start, count, stride):
    return jnp.concatenate(
        [ref[t, pl.ds(start, count, stride=stride), :] for t in range(ref.shape[0])], axis=1
    )


def turn_response(response, b_ref, y_ref, h_ref):
    shots, rows_e, taps = response.shape
    per_tile = LANES // shots
    tiles = taps // per_tile
    b_ref[:, :taps] = response.astype(jnp.float32).reshape(shots * rows_e, taps)
    stacked = jnp.concatenate(
        [b_ref[pl.ds(k, shots, stride=rows_e), :] for k in range(rows_e)], axis=0
    )
    put(y_ref, stacked.T[:taps])
    by_tap = [get_rows(y_ref, m, tiles, per_tile) for m in range(per_tile)]
    for k in range(rows_e):
        h_ref[pl.ds(k, tiles, stride=rows_e), :] = jnp.concatenate(
            [v[:, k * shots : (k + 1) * shots] for v in by_tap], axis=1
        )
    return h_ref[...].astype(jnp.bfloat16)


def turn_traces(traces, phases, a_ref, z_ref, w_ref):
    rows_d, rcv, samples = traces.shape
    blocks = samples // phases
    put(a_ref, traces.astype(jnp.float32).reshape(rows_d * rcv, samples))
    stacked = jnp.concatenate([get_rows(a_ref, r, rows_d, rcv) for r in range(rcv)], axis=0)
    put(z_ref, stacked.T)
    by_phase = [get_rows(z_ref, v, blocks, phases) for v in range(phases)]
    for r in range(rcv):
        row = jnp.concatenate([z[:, r * rows_d : (r + 1) * rows_d] for z in by_phase], axis=1)
        put_rows(w_ref, r, blocks, rcv, row)
    return get(w_ref).astype(jnp.bfloat16)


def arrange(y_ref, o_ref, acc, z_ref, f_ref):
    shots, rcv, samples = o_ref.shape
    phases = WIDTH // shots
    blocks = samples // phases
    put(acc, y_ref[...].astype(jnp.float32))
    by_rcv = [get_rows(acc, r, blocks, rcv) for r in range(rcv)]
    for u in range(phases):
        row = jnp.concatenate([v[:, u * shots : (u + 1) * shots] for v in by_rcv], axis=1)
        put_rows(z_ref, u, blocks, phases, row)
    turned = get(z_ref).T
    for r in range(rcv):
        put_rows(f_ref, r, shots, rcv, turned[r * shots : (r + 1) * shots])
    o_ref[...] = get(f_ref).reshape(shots, rcv, samples).astype(jnp.bfloat16)


def predict(
    n_shot, n_rcv, chunks,
    response_hbm, traces_hbm, o_ref,
    response_ref, traces_ref, b_ref, y_ref, h_ref, a_ref, z_ref, w_ref,
    x_ref, g_ref, xland, gland, bands, even, odd, acc,
    load, xsend, xrecv, xfwd, gsend, grecv, gfwd,
):
    shots, rows_e, taps = response_ref.shape
    rows_d, rcv, samples = traces_ref.shape
    rows, width = x_ref.shape
    phases = WIDTH // shots
    per_tile = LANES // shots
    tiles = taps // per_tile
    pad = phases // per_tile
    history = taps // phases
    ratio = rows_d // rows_e
    head = history * rcv
    half = rows // 2
    outer_d, outer_e = n_shot // 2, n_rcv // 2
    me_d, me_e = lax.axis_index("shot"), lax.axis_index("rcv")
    in_d, in_e = lax.rem(me_d, 2), lax.rem(me_e, 2)
    out_d, out_e = me_d // 2, me_e // 2
    mate_d = out_d * 2 + 1 - in_d
    mate_e = out_e * 2 + 1 - in_e

    def at_d(step):
        return lax.rem(out_d + step + outer_d, outer_d) * 2 + in_d

    def at_e(step):
        return lax.rem(out_e + step + outer_e, outer_e) * 2 + in_e

    barrier = pltpu.get_barrier_semaphore()
    peers = [(mate_d, me_e), (me_d, mate_e)]
    peers += [(at_d(i), me_e) for i in range(1, outer_d)]
    peers += [(me_d, at_e(i)) for i in range(1, outer_e)]
    for peer in peers:
        pl.semaphore_signal(barrier, inc=1, device_id=peer, device_id_type=MESH)
    fetch_r = pltpu.make_async_copy(response_hbm, response_ref, load.at[0])
    fetch_t = pltpu.make_async_copy(traces_hbm, traces_ref, load.at[1])
    fetch_r.start()
    fetch_t.start()

    part = rows // chunks

    def xcopy(src, owner, c, send, peer):
        piece = pl.ds(c * part, part)
        return pltpu.make_async_remote_copy(
            src_ref=src.at[piece],
            dst_ref=xland.at[owner, piece],
            send_sem=send,
            recv_sem=xrecv.at[owner, c],
            device_id=peer,
            device_id_type=MESH,
        )

    def gcopy(src, owner, send, peer):
        return pltpu.make_async_remote_copy(
            src_ref=src,
            dst_ref=gland.at[owner],
            send_sem=send,
            recv_sem=grecv.at[owner],
            device_id=peer,
            device_id_type=MESH,
        )

    pending = []

    def go(copy):
        copy.start()
        pending.append(copy)

    fetch_r.wait()
    g_ref[...] = turn_response(response_ref[...], b_ref, y_ref, h_ref)
    pl.semaphore_wait(barrier, len(peers))
    order = sorted(range(1, outer_e), key=lambda i: abs(2 * i - outer_e))
    for i in order:
        go(gcopy(g_ref, me_e, gsend.at[i], (me_d, at_e(i))))
    go(gcopy(g_ref, me_e, gsend.at[0], (me_d, mate_e)))
    fetch_t.wait()
    span = samples // chunks
    for c in range(chunks + 1):
        if c < chunks:
            x_ref[pl.ds(c * part, part), :] = turn_traces(
                traces_ref[:, :, pl.ds(c * span, span)], phases, a_ref, z_ref, w_ref
            )
        if c > 0:
            for i in range(1, outer_d):
                go(xcopy(x_ref, me_d, c - 1, xsend.at[i, c - 1], (at_d(i), me_e)))
    for c in range(chunks):
        go(xcopy(x_ref, me_d, c, xsend.at[0, c], (mate_d, me_e)))

    blank = jnp.zeros((rows_e, LANES), jnp.bfloat16)

    def build(e, held):
        padded = [blank] * pad
        padded += [held[a * rows_e : (a + 1) * rows_e] for a in range(tiles)]
        padded += [blank] * (pad + 1)
        for a in range(tiles + 2 * pad):
            for q in range(per_tile):
                value = padded[a]
                if q > 0:
                    value = jnp.concatenate(
                        [padded[a][:, q * shots :], padded[a + 1][:, : q * shots]], axis=1
                    )
                bands[e, q, a] = value

    def place(owner, held, h):
        even[owner, pl.ds(head + h * half, half), :] = held
        odd[owner, pl.ds(head - rcv + h * half, half), :] = held

    def add(owner, h, first=False, last=False):
        left, right = [], []
        for v1 in range(history + 1):
            if v1 % 2 == 0:
                left.append(even[owner, pl.ds(h * half + v1 * rcv, half), :])
            else:
                left.append(odd[owner, pl.ds(h * half + (v1 - 1) * rcv, half), :])
            for v0 in range(phases):
                start = taps - v1 * phases - v0 + phases
                a, q = start // per_tile, start % per_tile
                for k in range(ratio):
                    e = owner * ratio + k
                    right.append(
                        jnp.concatenate([bands[e, q, a + n] for n in range(pad)], axis=1)
                    )
        total = jnp.dot(
            jnp.concatenate(left, axis=1),
            jnp.concatenate(right, axis=0),
            preferred_element_type=jnp.float32,
        )
        mine = pl.ds(h * half, half)
        if not first:
            total = acc[mine, :] + total
        if last:
            o_ref[mine, :] = total.astype(jnp.bfloat16)
        else:
            acc[mine, :] = total

    def forward_x(i, c):
        owner = at_d(-i)
        copy = xcopy(xland.at[owner], owner, c, xfwd.at[i, c], (mate_d, me_e))
        copy.wait_recv()
        go(copy)

    for d in range(n_shot):
        even[d, pl.ds(0, head), :] = jnp.zeros((head, width), jnp.bfloat16)
        odd[d, pl.ds(0, head), :] = jnp.zeros((head, width), jnp.bfloat16)
    for h in range(2):
        place(me_d, x_ref[pl.ds(h * half, half), :], h)
    build(me_e, g_ref[...])

    def arrived(h):
        for i in range(outer_d):
            owner = lax.rem(out_d - i + outer_d, outer_d) * 2 + 1 - in_d
            for c in range(h * chunks // 2, (h + 1) * chunks // 2):
                xcopy(x_ref, owner, c, xsend.at[0, c], (mate_d, me_e)).wait_recv()
            place(owner, xland[owner, pl.ds(h * half, half), :], h)
            if i > 0:
                owner = at_d(-i)
                place(owner, xland[owner, pl.ds(h * half, half), :], h)

    todo = [(i, c) for c in range(chunks) for i in range(1, outer_d)]
    late = todo[len(todo) // 2 :]
    todo = todo[: len(todo) // 2]
    for n in range(max(outer_e - 1, len(todo))):
        if n < outer_e - 1:
            owner = at_e(-order[n])
            copy = gcopy(gland.at[owner], owner, gfwd.at[n], (me_d, mate_e))
            copy.wait_recv()
            go(copy)
        if n < len(todo):
            forward_x(*todo[n])
        if n < outer_e - 1:
            build(owner, gland[owner])
    arrived(0)

    groups = [lax.rem(out_e - i + outer_e, outer_e) for i in [0] + order]
    early = ratio == 2 and outer_e - 1 >= len(late)
    if not early:
        for t in late:
            forward_x(*t)
    for n, group in enumerate(groups):
        if early and n == outer_e - 1:
            arrived(1)
            for m in range(n):
                add(groups[m], 1, first=m == 0)
        owner = group * 2 + 1 - in_e
        gcopy(g_ref, owner, gsend.at[0], (me_d, mate_e)).wait_recv()
        build(owner, gland[owner])
        if early:
            add(group, 0, first=n == 0, last=n == outer_e - 1)
            if n < len(late):
                forward_x(*late[n])
    if early:
        add(groups[-1], 1, last=True)
    else:
        arrived(1)
        for d in range(n_shot):
            for h in range(2):
                add(d, h, first=d == 0, last=d == n_shot - 1)
    for copy in pending:
        copy.wait_send()


def shards(n_shot, n_rcv, response, traces):
    shots, rows_e, taps = response.shape
    rows_d, rcv, samples = traces.shape
    phases = WIDTH // shots
    blocks = samples // phases
    per_tile = LANES // shots
    tiles = taps // per_tile
    pad = phases // per_tile
    rows = blocks * rcv
    width = phases * rows_d
    chunks = 4
    f32, bf16 = jnp.float32, jnp.bfloat16

    def tiled(height, across):
        return pltpu.VMEM((across // LANES, height, LANES), f32)

    vmem = pl.BlockSpec(memory_space=pltpu.VMEM)
    outer_d, outer_e = n_shot // 2, n_rcv // 2
    head = taps // phases * rcv
    dma = pltpu.SemaphoreType.DMA
    y = pl.pallas_call(
        functools.partial(predict, n_shot, n_rcv, chunks),
        out_shape=jax.ShapeDtypeStruct((rows, WIDTH), bf16),
        in_specs=[pl.BlockSpec(memory_space=pl.ANY)] * 2,
        out_specs=vmem,
        scratch_shapes=[
            pltpu.VMEM(response.shape, bf16),
            pltpu.VMEM(traces.shape, bf16),
            pltpu.VMEM((shots * rows_e, LANES), f32),
            tiled(taps, rows_e * shots),
            pltpu.VMEM((tiles * rows_e, LANES), f32),
            tiled(rows_d * rcv, samples // chunks),
            tiled(samples // chunks, rcv * rows_d),
            tiled(rows // chunks, width),
            pltpu.VMEM((rows, width), bf16),
            pltpu.VMEM((tiles * rows_e, LANES), bf16),
            pltpu.VMEM((n_shot, rows, width), bf16),
            pltpu.VMEM((n_rcv, tiles * rows_e, LANES), bf16),
            pltpu.VMEM((n_rcv, per_tile, tiles + 2 * pad, rows_e, LANES), bf16),
            pltpu.VMEM((n_shot, rows + head, width), bf16),
            pltpu.VMEM((n_shot, rows + head, width), bf16),
            pltpu.VMEM((rows, WIDTH), f32),
            dma((2,)),
            dma((outer_d, chunks)),
            dma((n_shot, chunks)),
            dma((outer_d, chunks)),
            dma((outer_e,)),
            dma((n_rcv,)),
            dma((outer_e,)),
        ],
        compiler_params=pltpu.CompilerParams(collective_id=0, has_side_effects=True),
    )(response, traces)
    return pl.pallas_call(
        arrange,
        out_shape=jax.ShapeDtypeStruct((shots, rcv, samples), bf16),
        in_specs=[vmem],
        out_specs=vmem,
        scratch_shapes=[
            tiled(rows, WIDTH),
            tiled(samples, rcv * shots),
            tiled(shots * rcv, samples),
        ],
    )(y)


def solution(mesh):
    placed = P("shot", "rcv", None)
    return jax.shard_map(
        functools.partial(shards, mesh.shape["shot"], mesh.shape["rcv"]),
        mesh=mesh, in_specs=(placed, placed), out_specs=placed, check_vma=False,
    )
```

```python
import functools

import jax
import jax.numpy as jnp
from jax import lax
from jax.experimental import pallas as pl
from jax.experimental.pallas import tpu as pltpu
from jax.sharding import PartitionSpec as P

MESH = pl.DeviceIdType.MESH
LANES = 128
WIDTH = 256


def put(ref, value):
    for t in range(value.shape[1] // LANES):
        ref[t] = value[:, t * LANES : (t + 1) * LANES]


def put_rows(ref, start, count, stride, value):
    for t in range(value.shape[1] // LANES):
        ref[t, pl.ds(start, count, stride=stride), :] = value[:, t * LANES : (t + 1) * LANES]


def get(ref):
    return jnp.concatenate([ref[t] for t in range(ref.shape[0])], axis=1)


def get_rows(ref, start, count, stride):
    return jnp.concatenate(
        [ref[t, pl.ds(start, count, stride=stride), :] for t in range(ref.shape[0])], axis=1
    )


def turn_response(response, b_ref, y_ref, h_ref):
    shots, rows_e, taps = response.shape
    per_tile = LANES // shots
    tiles = taps // per_tile
    b_ref[:, :taps] = response.astype(jnp.float32).reshape(shots * rows_e, taps)
    stacked = jnp.concatenate(
        [b_ref[pl.ds(k, shots, stride=rows_e), :] for k in range(rows_e)], axis=0
    )
    put(y_ref, stacked.T[:taps])
    by_tap = [get_rows(y_ref, m, tiles, per_tile) for m in range(per_tile)]
    for k in range(rows_e):
        h_ref[pl.ds(k, tiles, stride=rows_e), :] = jnp.concatenate(
            [v[:, k * shots : (k + 1) * shots] for v in by_tap], axis=1
        )
    return h_ref[...].astype(jnp.bfloat16)


def turn_traces(traces, phases, a_ref, z_ref, w_ref):
    rows_d, rcv, samples = traces.shape
    blocks = samples // phases
    put(a_ref, traces.astype(jnp.float32).reshape(rows_d * rcv, samples))
    stacked = jnp.concatenate([get_rows(a_ref, r, rows_d, rcv) for r in range(rcv)], axis=0)
    put(z_ref, stacked.T)
    by_phase = [get_rows(z_ref, v, blocks, phases) for v in range(phases)]
    for r in range(rcv):
        row = jnp.concatenate([z[:, r * rows_d : (r + 1) * rows_d] for z in by_phase], axis=1)
        put_rows(w_ref, r, blocks, rcv, row)
    return get(w_ref).astype(jnp.bfloat16)


def arrange(y_ref, o_ref, acc, z_ref, f_ref):
    shots, rcv, samples = o_ref.shape
    phases = WIDTH // shots
    blocks = samples // phases
    put(acc, y_ref[...].astype(jnp.float32))
    by_rcv = [get_rows(acc, r, blocks, rcv) for r in range(rcv)]
    for u in range(phases):
        row = jnp.concatenate([v[:, u * shots : (u + 1) * shots] for v in by_rcv], axis=1)
        put_rows(z_ref, u, blocks, phases, row)
    turned = get(z_ref).T
    for r in range(rcv):
        put_rows(f_ref, r, shots, rcv, turned[r * shots : (r + 1) * shots])
    o_ref[...] = get(f_ref).reshape(shots, rcv, samples).astype(jnp.bfloat16)


def predict(
    n_shot, n_rcv, chunks,
    response_hbm, traces_hbm, o_ref,
    response_ref, traces_ref, b_ref, y_ref, h_ref, a_ref, z_ref, w_ref,
    x_ref, g_ref, xland, gland, bands, even, odd, acc,
    load, xsend, xrecv, xfwd, gsend, grecv, gfwd,
):
    shots, rows_e, taps = response_ref.shape
    rows_d, rcv, samples = traces_ref.shape
    rows, width = x_ref.shape
    phases = WIDTH // shots
    per_tile = LANES // shots
    tiles = taps // per_tile
    pad = phases // per_tile
    history = taps // phases
    ratio = rows_d // rows_e
    head = history * rcv
    half = rows // 2
    outer_d, outer_e = n_shot // 2, n_rcv // 2
    me_d, me_e = lax.axis_index("shot"), lax.axis_index("rcv")
    in_d, in_e = lax.rem(me_d, 2), lax.rem(me_e, 2)
    out_d, out_e = me_d // 2, me_e // 2
    mate_d = out_d * 2 + 1 - in_d
    mate_e = out_e * 2 + 1 - in_e

    def at_d(step):
        return lax.rem(out_d + step + outer_d, outer_d) * 2 + in_d

    def at_e(step):
        return lax.rem(out_e + step + outer_e, outer_e) * 2 + in_e

    barrier = pltpu.get_barrier_semaphore()
    peers = [(mate_d, me_e), (me_d, mate_e)]
    peers += [(at_d(i), me_e) for i in range(1, outer_d)]
    peers += [(me_d, at_e(i)) for i in range(1, outer_e)]
    for peer in peers:
        pl.semaphore_signal(barrier, inc=1, device_id=peer, device_id_type=MESH)
    fetch_r = pltpu.make_async_copy(response_hbm, response_ref, load.at[0])
    fetch_t = pltpu.make_async_copy(traces_hbm, traces_ref, load.at[1])
    fetch_r.start()
    fetch_t.start()

    part = rows // chunks

    def xcopy(src, owner, c, send, peer):
        piece = pl.ds(c * part, part)
        return pltpu.make_async_remote_copy(
            src_ref=src.at[piece],
            dst_ref=xland.at[owner, piece],
            send_sem=send,
            recv_sem=xrecv.at[owner, c],
            device_id=peer,
            device_id_type=MESH,
        )

    def gcopy(src, owner, send, peer):
        return pltpu.make_async_remote_copy(
            src_ref=src,
            dst_ref=gland.at[owner],
            send_sem=send,
            recv_sem=grecv.at[owner],
            device_id=peer,
            device_id_type=MESH,
        )

    pending = []

    def go(copy):
        copy.start()
        pending.append(copy)

    fetch_r.wait()
    g_ref[...] = turn_response(response_ref[...], b_ref, y_ref, h_ref)
    pl.semaphore_wait(barrier, len(peers))
    order = sorted(range(1, outer_e), key=lambda i: abs(2 * i - outer_e))
    for i in order:
        go(gcopy(g_ref, me_e, gsend.at[i], (me_d, at_e(i))))
    go(gcopy(g_ref, me_e, gsend.at[0], (me_d, mate_e)))
    fetch_t.wait()
    span = samples // chunks
    for c in range(chunks + 1):
        if c < chunks:
            x_ref[pl.ds(c * part, part), :] = turn_traces(
                traces_ref[:, :, pl.ds(c * span, span)], phases, a_ref, z_ref, w_ref
            )
        if c > 0:
            for i in range(1, outer_d):
                go(xcopy(x_ref, me_d, c - 1, xsend.at[i, c - 1], (at_d(i), me_e)))
    for c in range(chunks):
        go(xcopy(x_ref, me_d, c, xsend.at[0, c], (mate_d, me_e)))

    blank = jnp.zeros((rows_e, LANES), jnp.bfloat16)

    def build(e, held):
        padded = [blank] * pad
        padded += [held[a * rows_e : (a + 1) * rows_e] for a in range(tiles)]
        padded += [blank] * (pad + 1)
        for a in range(tiles + 2 * pad):
            for q in range(per_tile):
                value = padded[a]
                if q > 0:
                    value = jnp.concatenate(
                        [padded[a][:, q * shots :], padded[a + 1][:, : q * shots]], axis=1
                    )
                bands[e, q, a] = value

    def place(owner, held, h):
        even[owner, pl.ds(head + h * half, half), :] = held
        odd[owner, pl.ds(head - rcv + h * half, half), :] = held

    def add(owner, h, first=False, last=False):
        left, right = [], []
        for v1 in range(history + 1):
            if v1 % 2 == 0:
                left.append(even[owner, pl.ds(h * half + v1 * rcv, half), :])
            else:
                left.append(odd[owner, pl.ds(h * half + (v1 - 1) * rcv, half), :])
            for v0 in range(phases):
                start = taps - v1 * phases - v0 + phases
                a, q = start // per_tile, start % per_tile
                for k in range(ratio):
                    e = owner * ratio + k
                    right.append(
                        jnp.concatenate([bands[e, q, a + n] for n in range(pad)], axis=1)
                    )
        total = jnp.dot(
            jnp.concatenate(left, axis=1),
            jnp.concatenate(right, axis=0),
            preferred_element_type=jnp.float32,
        )
        mine = pl.ds(h * half, half)
        if not first:
            total = acc[mine, :] + total
        if last:
            o_ref[mine, :] = total.astype(jnp.bfloat16)
        else:
            acc[mine, :] = total

    def forward_x(i, c):
        owner = at_d(-i)
        copy = xcopy(xland.at[owner], owner, c, xfwd.at[i, c], (mate_d, me_e))
        copy.wait_recv()
        go(copy)

    for d in range(n_shot):
        even[d, pl.ds(0, head), :] = jnp.zeros((head, width), jnp.bfloat16)
        odd[d, pl.ds(0, head), :] = jnp.zeros((head, width), jnp.bfloat16)
    for h in range(2):
        place(me_d, x_ref[pl.ds(h * half, half), :], h)
    build(me_e, g_ref[...])

    def arrived(owner):
        for c in range(chunks):
            xcopy(x_ref, owner, c, xsend.at[0, c], (mate_d, me_e)).wait_recv()

    def bring(owner):
        for h in range(2):
            place(owner, xland[owner, pl.ds(h * half, half), :], h)

    todo = [(i, c) for c in range(chunks) for i in range(1, outer_d)]
    for n in range(max(outer_e - 1, len(todo))):
        if n < len(todo):
            forward_x(*todo[n])
        if n < outer_e - 1:
            owner = at_e(-order[n])
            copy = gcopy(gland.at[owner], owner, gfwd.at[n], (me_d, mate_e))
            copy.wait_recv()
            go(copy)
        if n < outer_e - 1:
            build(owner, gland[owner])
    arrived(mate_d)
    bring(mate_d)
    for i in range(1, outer_d):
        bring(at_d(-i))
    for i in range(1, outer_d):
        owner = lax.rem(out_d - i + outer_d, outer_d) * 2 + 1 - in_d
        arrived(owner)
        bring(owner)

    for n, i in enumerate([0] + order):
        group = lax.rem(out_e - i + outer_e, outer_e)
        owner = group * 2 + 1 - in_e
        gcopy(g_ref, owner, gsend.at[0], (me_d, mate_e)).wait_recv()
        build(owner, gland[owner])
        if ratio == 2:
            for h in range(2):
                add(group, h, first=n == 0, last=n == outer_e - 1)
    if ratio != 2:
        for d in range(n_shot):
            for h in range(2):
                add(d, h, first=d == 0, last=d == n_shot - 1)
    for copy in pending:
        copy.wait_send()


def shards(n_shot, n_rcv, response, traces):
    shots, rows_e, taps = response.shape
    rows_d, rcv, samples = traces.shape
    phases = WIDTH // shots
    blocks = samples // phases
    per_tile = LANES // shots
    tiles = taps // per_tile
    pad = phases // per_tile
    rows = blocks * rcv
    width = phases * rows_d
    chunks = 4
    f32, bf16 = jnp.float32, jnp.bfloat16

    def tiled(height, across):
        return pltpu.VMEM((across // LANES, height, LANES), f32)

    vmem = pl.BlockSpec(memory_space=pltpu.VMEM)
    outer_d, outer_e = n_shot // 2, n_rcv // 2
    head = taps // phases * rcv
    dma = pltpu.SemaphoreType.DMA
    y = pl.pallas_call(
        functools.partial(predict, n_shot, n_rcv, chunks),
        out_shape=jax.ShapeDtypeStruct((rows, WIDTH), bf16),
        in_specs=[pl.BlockSpec(memory_space=pl.ANY)] * 2,
        out_specs=vmem,
        scratch_shapes=[
            pltpu.VMEM(response.shape, bf16),
            pltpu.VMEM(traces.shape, bf16),
            pltpu.VMEM((shots * rows_e, LANES), f32),
            tiled(taps, rows_e * shots),
            pltpu.VMEM((tiles * rows_e, LANES), f32),
            tiled(rows_d * rcv, samples // chunks),
            tiled(samples // chunks, rcv * rows_d),
            tiled(rows // chunks, width),
            pltpu.VMEM((rows, width), bf16),
            pltpu.VMEM((tiles * rows_e, LANES), bf16),
            pltpu.VMEM((n_shot, rows, width), bf16),
            pltpu.VMEM((n_rcv, tiles * rows_e, LANES), bf16),
            pltpu.VMEM((n_rcv, per_tile, tiles + 2 * pad, rows_e, LANES), bf16),
            pltpu.VMEM((n_shot, rows + head, width), bf16),
            pltpu.VMEM((n_shot, rows + head, width), bf16),
            pltpu.VMEM((rows, WIDTH), f32),
            dma((2,)),
            dma((outer_d, chunks)),
            dma((n_shot, chunks)),
            dma((outer_d, chunks)),
            dma((outer_e,)),
            dma((n_rcv,)),
            dma((outer_e,)),
        ],
        compiler_params=pltpu.CompilerParams(collective_id=0, has_side_effects=True),
    )(response, traces)
    return pl.pallas_call(
        arrange,
        out_shape=jax.ShapeDtypeStruct((shots, rcv, samples), bf16),
        in_specs=[vmem],
        out_specs=vmem,
        scratch_shapes=[
            tiled(rows, WIDTH),
            tiled(samples, rcv * shots),
            tiled(shots * rcv, samples),
        ],
    )(y)


def solution(mesh):
    placed = P("shot", "rcv", None)
    return jax.shard_map(
        functools.partial(shards, mesh.shape["shot"], mesh.shape["rcv"]),
        mesh=mesh, in_specs=(placed, placed), out_specs=placed, check_vma=False,
    )
```

```python
import functools

import jax
import jax.numpy as jnp
from jax import lax
from jax.experimental import pallas as pl
from jax.experimental.pallas import tpu as pltpu
from jax.sharding import PartitionSpec as P

MESH = pl.DeviceIdType.MESH
LANES = 128
WIDTH = 256


def put(ref, value):
    for t in range(value.shape[1] // LANES):
        ref[t] = value[:, t * LANES : (t + 1) * LANES]


def put_rows(ref, start, count, stride, value):
    for t in range(value.shape[1] // LANES):
        ref[t, pl.ds(start, count, stride=stride), :] = value[:, t * LANES : (t + 1) * LANES]


def get(ref):
    return jnp.concatenate([ref[t] for t in range(ref.shape[0])], axis=1)


def get_rows(ref, start, count, stride):
    return jnp.concatenate(
        [ref[t, pl.ds(start, count, stride=stride), :] for t in range(ref.shape[0])], axis=1
    )


def turn_response(response, b_ref, y_ref, h_ref):
    shots, rows_e, taps = response.shape
    per_tile = LANES // shots
    tiles = taps // per_tile
    b_ref[:, :taps] = response.astype(jnp.float32).reshape(shots * rows_e, taps)
    stacked = jnp.concatenate(
        [b_ref[pl.ds(k, shots, stride=rows_e), :] for k in range(rows_e)], axis=0
    )
    put(y_ref, stacked.T[:taps])
    by_tap = [get_rows(y_ref, m, tiles, per_tile) for m in range(per_tile)]
    for k in range(rows_e):
        h_ref[pl.ds(k, tiles, stride=rows_e), :] = jnp.concatenate(
            [v[:, k * shots : (k + 1) * shots] for v in by_tap], axis=1
        )
    return h_ref[...].astype(jnp.bfloat16)


def turn_traces(traces, phases, a_ref, z_ref, w_ref):
    rows_d, rcv, samples = traces.shape
    blocks = samples // phases
    put(a_ref, traces.astype(jnp.float32).reshape(rows_d * rcv, samples))
    stacked = jnp.concatenate([get_rows(a_ref, r, rows_d, rcv) for r in range(rcv)], axis=0)
    put(z_ref, stacked.T)
    by_phase = [get_rows(z_ref, v, blocks, phases) for v in range(phases)]
    for r in range(rcv):
        row = jnp.concatenate([z[:, r * rows_d : (r + 1) * rows_d] for z in by_phase], axis=1)
        put_rows(w_ref, r, blocks, rcv, row)
    return get(w_ref).astype(jnp.bfloat16)


def arrange(y_ref, o_ref, acc, z_ref, f_ref):
    shots, rcv, samples = o_ref.shape
    phases = WIDTH // shots
    blocks = samples // phases
    put(acc, y_ref[...].astype(jnp.float32))
    by_rcv = [get_rows(acc, r, blocks, rcv) for r in range(rcv)]
    for u in range(phases):
        row = jnp.concatenate([v[:, u * shots : (u + 1) * shots] for v in by_rcv], axis=1)
        put_rows(z_ref, u, blocks, phases, row)
    turned = get(z_ref).T
    for r in range(rcv):
        put_rows(f_ref, r, shots, rcv, turned[r * shots : (r + 1) * shots])
    o_ref[...] = get(f_ref).reshape(shots, rcv, samples).astype(jnp.bfloat16)


def predict(
    n_shot, n_rcv, chunks,
    response_hbm, traces_hbm, o_ref,
    response_ref, traces_ref, b_ref, y_ref, h_ref, a_ref, z_ref, w_ref,
    x_ref, g_ref, xland, gland, bands, even, odd, acc,
    load, xsend, xrecv, xfwd, gsend, grecv, gfwd,
):
    shots, rows_e, taps = response_ref.shape
    rows_d, rcv, samples = traces_ref.shape
    rows, width = x_ref.shape
    phases = WIDTH // shots
    per_tile = LANES // shots
    tiles = taps // per_tile
    pad = phases // per_tile
    history = taps // phases
    ratio = rows_d // rows_e
    head = history * rcv
    half = rows // 2
    outer_d, outer_e = n_shot // 2, n_rcv // 2
    me_d, me_e = lax.axis_index("shot"), lax.axis_index("rcv")
    in_d, in_e = lax.rem(me_d, 2), lax.rem(me_e, 2)
    out_d, out_e = me_d // 2, me_e // 2
    mate_d = out_d * 2 + 1 - in_d
    mate_e = out_e * 2 + 1 - in_e

    def at_d(step):
        return lax.rem(out_d + step + outer_d, outer_d) * 2 + in_d

    def at_e(step):
        return lax.rem(out_e + step + outer_e, outer_e) * 2 + in_e

    barrier = pltpu.get_barrier_semaphore()
    peers = [(mate_d, me_e), (me_d, mate_e)]
    peers += [(at_d(i), me_e) for i in range(1, outer_d)]
    peers += [(me_d, at_e(i)) for i in range(1, outer_e)]
    for peer in peers:
        pl.semaphore_signal(barrier, inc=1, device_id=peer, device_id_type=MESH)
    fetch_r = pltpu.make_async_copy(response_hbm, response_ref, load.at[0])
    fetch_t = pltpu.make_async_copy(traces_hbm, traces_ref, load.at[1])
    fetch_r.start()
    fetch_t.start()

    part = rows // chunks

    def xcopy(src, owner, c, send, peer):
        piece = pl.ds(c * part, part)
        return pltpu.make_async_remote_copy(
            src_ref=src.at[piece],
            dst_ref=xland.at[owner, piece],
            send_sem=send,
            recv_sem=xrecv.at[owner, c],
            device_id=peer,
            device_id_type=MESH,
        )

    def gcopy(src, owner, send, peer):
        return pltpu.make_async_remote_copy(
            src_ref=src,
            dst_ref=gland.at[owner],
            send_sem=send,
            recv_sem=grecv.at[owner],
            device_id=peer,
            device_id_type=MESH,
        )

    pending = []

    def go(copy):
        copy.start()
        pending.append(copy)

    fetch_r.wait()
    g_ref[...] = turn_response(response_ref[...], b_ref, y_ref, h_ref)
    pl.semaphore_wait(barrier, len(peers))
    order = sorted(range(1, outer_e), key=lambda i: abs(2 * i - outer_e))
    for i in order:
        go(gcopy(g_ref, me_e, gsend.at[i], (me_d, at_e(i))))
    go(gcopy(g_ref, me_e, gsend.at[0], (me_d, mate_e)))
    fetch_t.wait()
    span = samples // chunks
    for c in range(chunks + 1):
        if c < chunks:
            x_ref[pl.ds(c * part, part), :] = turn_traces(
                traces_ref[:, :, pl.ds(c * span, span)], phases, a_ref, z_ref, w_ref
            )
        if c > 0:
            for i in range(1, outer_d):
                go(xcopy(x_ref, me_d, c - 1, xsend.at[i, c - 1], (at_d(i), me_e)))
    for c in range(chunks):
        go(xcopy(x_ref, me_d, c, xsend.at[0, c], (mate_d, me_e)))

    blank = jnp.zeros((rows_e, LANES), jnp.bfloat16)

    def build(e, held):
        padded = [blank] * pad
        padded += [held[a * rows_e : (a + 1) * rows_e] for a in range(tiles)]
        padded += [blank] * (pad + 1)
        for a in range(tiles + 2 * pad):
            for q in range(per_tile):
                value = padded[a]
                if q > 0:
                    value = jnp.concatenate(
                        [padded[a][:, q * shots :], padded[a + 1][:, : q * shots]], axis=1
                    )
                bands[e, q, a] = value

    def place(owner, held, h):
        even[owner, pl.ds(head + h * half, half), :] = held
        odd[owner, pl.ds(head - rcv + h * half, half), :] = held

    def add(owner, h, first=False, last=False):
        left, right = [], []
        for v1 in range(history + 1):
            if v1 % 2 == 0:
                left.append(even[owner, pl.ds(h * half + v1 * rcv, half), :])
            else:
                left.append(odd[owner, pl.ds(h * half + (v1 - 1) * rcv, half), :])
            for v0 in range(phases):
                start = taps - v1 * phases - v0 + phases
                a, q = start // per_tile, start % per_tile
                for k in range(ratio):
                    e = owner * ratio + k
                    right.append(
                        jnp.concatenate([bands[e, q, a + n] for n in range(pad)], axis=1)
                    )
        total = jnp.dot(
            jnp.concatenate(left, axis=1),
            jnp.concatenate(right, axis=0),
            preferred_element_type=jnp.float32,
        )
        mine = pl.ds(h * half, half)
        if not first:
            total = acc[mine, :] + total
        if last:
            o_ref[mine, :] = total.astype(jnp.bfloat16)
        else:
            acc[mine, :] = total

    def forward_x(i, c):
        owner = at_d(-i)
        copy = xcopy(xland.at[owner], owner, c, xfwd.at[i, c], (mate_d, me_e))
        copy.wait_recv()
        go(copy)

    for d in range(n_shot):
        even[d, pl.ds(0, head), :] = jnp.zeros((head, width), jnp.bfloat16)
        odd[d, pl.ds(0, head), :] = jnp.zeros((head, width), jnp.bfloat16)
    for h in range(2):
        place(me_d, x_ref[pl.ds(h * half, half), :], h)
    build(me_e, g_ref[...])

    def arrived(owner):
        for c in range(chunks):
            xcopy(x_ref, owner, c, xsend.at[0, c], (mate_d, me_e)).wait_recv()

    def bring(owner):
        for h in range(2):
            place(owner, xland[owner, pl.ds(h * half, half), :], h)

    todo = [(i, c) for c in range(chunks) for i in range(1, outer_d)]
    for n in range(max(outer_e - 1, len(todo))):
        if n < len(todo):
            forward_x(*todo[n])
        if n < outer_e - 1:
            owner = at_e(-order[n])
            copy = gcopy(gland.at[owner], owner, gfwd.at[n], (me_d, mate_e))
            copy.wait_recv()
            go(copy)
        if n < outer_e - 1:
            build(owner, gland[owner])
    def meet(group):
        owner = group * 2 + 1 - in_e
        gcopy(g_ref, owner, gsend.at[0], (me_d, mate_e)).wait_recv()
        build(owner, gland[owner])

    meet(out_e)
    arrived(mate_d)
    bring(mate_d)
    for i in range(1, outer_d):
        bring(at_d(-i))
    for i in range(1, outer_d):
        owner = lax.rem(out_d - i + outer_d, outer_d) * 2 + 1 - in_d
        arrived(owner)
        bring(owner)

    for n, i in enumerate([0] + order):
        group = lax.rem(out_e - i + outer_e, outer_e)
        if n > 0:
            meet(group)
        if ratio == 2:
            for h in range(2):
                add(group, h, first=n == 0, last=n == outer_e - 1)
    if ratio != 2:
        for d in range(n_shot):
            for h in range(2):
                add(d, h, first=d == 0, last=d == n_shot - 1)
    for copy in pending:
        copy.wait_send()


def shards(n_shot, n_rcv, response, traces):
    shots, rows_e, taps = response.shape
    rows_d, rcv, samples = traces.shape
    phases = WIDTH // shots
    blocks = samples // phases
    per_tile = LANES // shots
    tiles = taps // per_tile
    pad = phases // per_tile
    rows = blocks * rcv
    width = phases * rows_d
    chunks = 4
    f32, bf16 = jnp.float32, jnp.bfloat16

    def tiled(height, across):
        return pltpu.VMEM((across // LANES, height, LANES), f32)

    vmem = pl.BlockSpec(memory_space=pltpu.VMEM)
    outer_d, outer_e = n_shot // 2, n_rcv // 2
    head = taps // phases * rcv
    dma = pltpu.SemaphoreType.DMA
    y = pl.pallas_call(
        functools.partial(predict, n_shot, n_rcv, chunks),
        out_shape=jax.ShapeDtypeStruct((rows, WIDTH), bf16),
        in_specs=[pl.BlockSpec(memory_space=pl.ANY)] * 2,
        out_specs=vmem,
        scratch_shapes=[
            pltpu.VMEM(response.shape, bf16),
            pltpu.VMEM(traces.shape, bf16),
            pltpu.VMEM((shots * rows_e, LANES), f32),
            tiled(taps, rows_e * shots),
            pltpu.VMEM((tiles * rows_e, LANES), f32),
            tiled(rows_d * rcv, samples // chunks),
            tiled(samples // chunks, rcv * rows_d),
            tiled(rows // chunks, width),
            pltpu.VMEM((rows, width), bf16),
            pltpu.VMEM((tiles * rows_e, LANES), bf16),
            pltpu.VMEM((n_shot, rows, width), bf16),
            pltpu.VMEM((n_rcv, tiles * rows_e, LANES), bf16),
            pltpu.VMEM((n_rcv, per_tile, tiles + 2 * pad, rows_e, LANES), bf16),
            pltpu.VMEM((n_shot, rows + head, width), bf16),
            pltpu.VMEM((n_shot, rows + head, width), bf16),
            pltpu.VMEM((rows, WIDTH), f32),
            dma((2,)),
            dma((outer_d, chunks)),
            dma((n_shot, chunks)),
            dma((outer_d, chunks)),
            dma((outer_e,)),
            dma((n_rcv,)),
            dma((outer_e,)),
        ],
        compiler_params=pltpu.CompilerParams(collective_id=0, has_side_effects=True),
    )(response, traces)
    return pl.pallas_call(
        arrange,
        out_shape=jax.ShapeDtypeStruct((shots, rcv, samples), bf16),
        in_specs=[vmem],
        out_specs=vmem,
        scratch_shapes=[
            tiled(rows, WIDTH),
            tiled(samples, rcv * shots),
            tiled(shots * rcv, samples),
        ],
    )(y)


def solution(mesh):
    placed = P("shot", "rcv", None)
    return jax.shard_map(
        functools.partial(shards, mesh.shape["shot"], mesh.shape["rcv"]),
        mesh=mesh, in_specs=(placed, placed), out_specs=placed, check_vma=False,
    )
```
